1024 devices in a mesh: dp: 32 (over z), pipe: 8 (over x, core), tensor: 4 (over y).
Axes of the slice: x: 4, y: 4, z: 32, core: 2. Of those that a mesh axis runs over, the one named last changes fastest.
Arguments:
- residual: bfloat16 [8, 2, 2048, 6144], P('pipe', None, 'dp', 'tensor'), may hold values from -6 to 6
- queries: bfloat16 [8, 2, 2048, 6144], P('pipe', None, 'dp', 'tensor'), may hold values from -6 to 6
- keys_values: bfloat16 [8, 2, 2, 2048, 6144], P('pipe', None, None, 'dp', 'tensor'), may hold values from -18 to 18
- global_kv: bfloat16 [8, 2, 2, 384, 6144], P('pipe', None, None, None, 'tensor'), may hold values from -6 to 6
- block_ids: int32 [8, 2, 32, 48], P('pipe', None, 'dp', 'tensor'), may hold values from 0 to 31, as said below
- lengths: int32 [8, 2], P('pipe'), may hold values from 8 to 32, as said below
- gain: bfloat16 [8, 2, 6144], P('pipe', None, 'tensor'), may hold values from 0.5 to 1.5
Outputs:
- normed: bfloat16 [8, 2, 2048, 6144], P('pipe', None, 'dp', 'tensor')
The draws below stay inside these ranges and needn't reach their ends.
Inputs may be any that keep to these rules, and one draw needn't show every extreme that they name: `block_ids`: for one section and direction, the random blocks of the 1 query block of one index of dp in the 12 heads of one index of tensor lie at most 1 in the 1 block of any one index of dp, and exactly 1 for some index. `lengths`: for each section one of the two micro-batches has all 32 blocks live.
All inputs are finite; a program needn't handle non-finite values.
Results may differ from the reference program's by a relative error of at most 0.0053.
Values may be sent and summed in bfloat16 or wider, within the bound.
A program may use at most 64 MiB of HBM per device.

```python
import math
import jax
import jax.numpy as jnp
from jax import lax

D = 6144
HEADS = 48
HD = 128
BLK = 64
GLOB = 384
SECTIONS = 8
QB_DEV = 1
NBLK = 32
TOKENS = 2048
HEADS_DEV = 12
CAP = 1
N_DP = 32
N_TENSOR = 4


def draw_residual(key, part):
    shape = (SECTIONS, 2, TOKENS, D)
    row_scale = jnp.exp(jax.random.uniform(jax.random.fold_in(key, 21), (SECTIONS, 2, TOKENS, 1), minval=math.log(0.03), maxval=math.log(0.3)))
    values = jax.random.truncated_normal(jax.random.fold_in(key, 22), -6.0, 6.0, shape)
    column_scale = 1.0 + 2.0 * jnp.arange(D, dtype=jnp.float32) / D
    return (values * row_scale * column_scale).astype(jnp.bfloat16)


def draw_queries(key, part):
    shape = (SECTIONS, 2, TOKENS, D)
    values = jax.random.truncated_normal(jax.random.fold_in(key, 11), -6.0, 6.0, shape)
    return values.astype(jnp.bfloat16)


def draw_keys_values(key, part):
    shape = (SECTIONS, 2, TOKENS, D)
    key_part = jax.random.truncated_normal(jax.random.fold_in(key, 31), -6.0, 6.0, shape)
    value_part = 3.0 * jax.random.truncated_normal(jax.random.fold_in(key, 32), -6.0, 6.0, shape)
    return jnp.stack([key_part, value_part], axis=1).astype(jnp.bfloat16)


def draw_block_ids(key, part):
    per_group = QB_DEV * HEADS_DEV
    slot_total = N_DP * CAP
    group_count = SECTIONS * 2 * N_DP * N_TENSOR
    priority = jax.random.randint(jax.random.fold_in(key, 3), (group_count, slot_total), 0, 65536)
    priority = priority * slot_total + jnp.arange(slot_total, dtype=jnp.int32)[None, :]
    chosen = jnp.argsort(priority, axis=1)[:, :per_group]
    owner_dev = chosen // CAP
    local_block = jax.random.randint(jax.random.fold_in(key, 4), (group_count, per_group), 0, QB_DEV)
    block_index = owner_dev * QB_DEV + local_block
    block_index = block_index.reshape(SECTIONS, 2, N_DP, N_TENSOR, QB_DEV, HEADS_DEV).transpose(0, 1, 2, 4, 3, 5)
    return block_index.reshape(SECTIONS, 2, NBLK, HEADS).astype(jnp.int32)


def draw_lengths(key, part):
    full_side = jax.random.randint(jax.random.fold_in(key, 5), (SECTIONS, 1), 0, 2)
    shorter = jax.random.randint(jax.random.fold_in(key, 6), (SECTIONS, 2), max(1, NBLK // 4), NBLK + 1)
    is_full = jnp.arange(2, dtype=jnp.int32)[None, :] == full_side
    return jnp.where(is_full, NBLK, shorter).astype(jnp.int32)


def levels(rng, dims, pieces, least, high):
    def one(dim, shards_of):
        steps = jax.random.uniform(jax.random.fold_in(jax.random.fold_in(rng, 6), dim), (shards_of,), jnp.float32, least / len(pieces), high / len(pieces))
        return jnp.repeat(jnp.exp(steps), dims[dim] // shards_of).reshape((-1,) + (1,) * (len(dims) - dim - 1))

    factor_of = one(*pieces[0])
    for cut in pieces[1:]:
        factor_of = factor_of * one(*cut)
    return factor_of


def normal_values(rng, dims, width, limit, shards=(), kind=jnp.bfloat16):
    values = jax.random.normal(rng, dims, jnp.float32) * width
    if len(shards) > 0:
        values = levels(rng, dims, shards, -0.22, 0.18) * values
    return jnp.clip(values, min=-limit, max=limit).astype(kind)


def setup_inputs(seed: int = 0) -> dict:
    key_list = jax.random.split(jax.random.key(seed), 8)
    residual = draw_residual(jax.random.fold_in(key_list[7], 71), 0)
    queries = draw_queries(jax.random.fold_in(key_list[7], 71), 0)
    keys_values = draw_keys_values(jax.random.fold_in(key_list[7], 71), 0)
    global_kv = normal_values(key_list[3], (SECTIONS, 2, 2, GLOB, D), 1.0, 6.0, ((0, 8), (4, 4)))
    block_ids = draw_block_ids(jax.random.fold_in(key_list[7], 71), 0)
    lengths = draw_lengths(jax.random.fold_in(key_list[7], 71), 0)
    gain = jnp.clip(1.0 + 0.1 * jax.random.normal(key_list[6], (SECTIONS, 2, D), jnp.float32), 0.5, 1.5).astype(jnp.bfloat16)
    return {"residual": residual, "queries": queries, "keys_values": keys_values, "global_kv": global_kv, "block_ids": block_ids, "lengths": lengths, "gain": gain}


epsilon = 1e-05

def single_head(operands, seq_blocks):
    query_head, key_head, value_head, gkey_head, gvalue_head, index_head = operands
    zero_block = jnp.zeros((1, BLK, HD), jnp.float32)
    key_padded = jnp.concatenate([zero_block, key_head, zero_block], axis=0)
    value_padded = jnp.concatenate([zero_block, value_head, zero_block], axis=0)
    window_keys = jnp.concatenate([key_padded[offset:offset + NBLK] for offset in range(3)], axis=1)
    window_values = jnp.concatenate([value_padded[offset:offset + NBLK] for offset in range(3)], axis=1)
    random_keys = key_head[index_head]
    random_values = value_head[index_head]
    window_scores = jnp.einsum('nbe,nke->nbk', query_head, window_keys)
    global_scores = jnp.einsum('nbe,ke->nbk', query_head, gkey_head)
    random_scores = jnp.einsum('nbe,nke->nbk', query_head, random_keys)
    scores = jnp.concatenate([window_scores, global_scores, random_scores], axis=2) * HD ** (-0.5)
    block_number = jnp.arange(NBLK, dtype=jnp.int32)
    near_index = block_number[:, None] + jnp.arange(3, dtype=jnp.int32)[None, :] - 1
    near_valid = jnp.repeat((near_index >= 0) & (near_index < seq_blocks), BLK, axis=1)
    global_valid = jnp.ones((NBLK, GLOB), jnp.bool_)
    random_valid = jnp.repeat((index_head < seq_blocks)[:, None], BLK, axis=1)
    key_valid = jnp.concatenate([near_valid, global_valid, random_valid], axis=1)[:, None, :]
    scores = jnp.where(key_valid, scores, -jnp.inf)
    largest = lax.optimization_barrier(jnp.max(scores, axis=2, keepdims=True))
    weights = jnp.exp(scores - largest)
    weights = (weights / lax.optimization_barrier(jnp.sum(weights, axis=2, keepdims=True))).astype(jnp.bfloat16)
    weights = lax.optimization_barrier(weights).astype(jnp.float32)
    near_end = 3 * BLK
    glob_end = near_end + GLOB
    context = jnp.einsum('nbk,nke->nbe', weights[:, :, :near_end], window_values)
    context = context + jnp.einsum('nbk,ke->nbe', weights[:, :, near_end:glob_end], gvalue_head)
    context = context + jnp.einsum('nbk,nke->nbe', weights[:, :, glob_end:], random_values)
    query_valid = (block_number < seq_blocks)[:, None, None]
    return jnp.where(query_valid, context, 0.0)

def head_major(array):
    return array.astype(jnp.float32).reshape(array.shape[0] // BLK, BLK, HEADS, HD).transpose(2, 0, 1, 3)

def section_layer(operands):
    state, query, pair, global_pair, block_index, seq_blocks = operands
    query_heads = head_major(query)
    key_heads = head_major(pair[0])
    value_heads = head_major(pair[1])
    gkey_heads = global_pair[0].astype(jnp.float32).reshape(GLOB, HEADS, HD).transpose(1, 0, 2)
    gvalue_heads = global_pair[1].astype(jnp.float32).reshape(GLOB, HEADS, HD).transpose(1, 0, 2)
    index_heads = block_index.T
    context = lax.map(lambda items: single_head(items, seq_blocks), (query_heads, key_heads, value_heads, gkey_heads, gvalue_heads, index_heads))
    context = context.transpose(1, 2, 0, 3).reshape(TOKENS, D)
    return (state.astype(jnp.float32) + context).astype(jnp.bfloat16)

def reference(residual, queries, keys_values, global_kv, block_ids, lengths, gain):
    pair_count = SECTIONS * 2
    flat_state = residual.reshape(pair_count, TOKENS, D)
    flat_query = queries.reshape(pair_count, TOKENS, D)
    flat_pair = keys_values.transpose(0, 2, 1, 3, 4).reshape(pair_count, 2, TOKENS, D)
    flat_global = global_kv.transpose(0, 2, 1, 3, 4).reshape(pair_count, 2, GLOB, D)
    flat_index = block_ids.reshape(pair_count, NBLK, HEADS)
    flat_length = lengths.reshape(pair_count)
    updated = lax.map(section_layer, (flat_state, flat_query, flat_pair, flat_global, flat_index, flat_length))
    updated = updated.reshape(SECTIONS, 2, TOKENS, D)
    zero_section = jnp.zeros((1, TOKENS, D), jnp.bfloat16)
    from_above = jnp.concatenate([updated[1:, 0], zero_section], axis=0)
    from_below = jnp.concatenate([zero_section, updated[:-1, 1]], axis=0)
    arrived = jnp.stack([from_above, from_below], axis=1)
    wide = arrived.astype(jnp.float32)
    inverse = lax.rsqrt(lax.optimization_barrier(jnp.sum(wide * wide, axis=3, keepdims=True)) / D + epsilon)
    normed = (wide * inverse * gain.astype(jnp.float32)[:, :, None, :]).astype(jnp.bfloat16)
    return normed
```

```python
import functools

import jax
import jax.numpy as jnp
from jax import lax
from jax.experimental import pallas as pl
from jax.experimental.pallas import tpu as pltpu
from jax.sharding import PartitionSpec as P

HD = 128
BLK = 64
EPSILON = 1e-05
REACH = 1
HIDDEN = 1e30
GROUP = 4
MESH = pl.DeviceIdType.MESH


def kernel(
    reach,
    ids,
    lens,
    res_hbm,
    q_hbm,
    kv_hbm,
    glob_hbm,
    gain_hbm,
    out,
    own,
    halo,
    q_v,
    glob_v,
    res_v,
    gain_v,
    want,
    table,
    table_s,
    send,
    send_half,
    recv,
    acc,
    row_max,
    row_sum,
    upd,
    squares,
    arrived,
    squares_in,
    own_sem,
    load_sem,
    want_sem,
    halo_send_sem,
    halo_recv_sem,
    tile_sem,
    tile_recv_sem,
    out_sem,
    in_sem,
):
    n = lax.axis_size("dp")
    sections = lax.axis_size("pipe")
    parts = lax.axis_size("tensor")
    me = lax.axis_index("dp")
    section = lax.axis_index("pipe")
    part = lax.axis_index("tensor")
    heads = q_v.shape[2] // HD
    group = GROUP if heads % GROUP == 0 else 1
    full = n // 2 - reach - 1
    scale = HD ** (-0.5)

    def ring(index):
        return lax.rem(index + 2 * n, n)

    def own_load(c, h):
        return pltpu.make_async_copy(
            kv_hbm.at[0, :, c, :, pl.ds(h * HD, HD)], own[c].at[h], own_sem.at[c, h]
        )

    loads = [
        pltpu.make_async_copy(q_hbm.at[0], q_v, load_sem.at[0]),
        pltpu.make_async_copy(glob_hbm.at[0], glob_v, load_sem.at[1]),
        pltpu.make_async_copy(res_hbm.at[0], res_v, load_sem.at[2]),
        pltpu.make_async_copy(gain_hbm.at[0], gain_v, load_sem.at[3]),
    ]
    for c in range(2):
        for h in range(heads):
            own_load(c, h).start()

    barrier = pltpu.get_barrier_semaphore()

    def greet(step, carry):
        pl.semaphore_signal(
            barrier, inc=1, device_id={"dp": ring(me + step)}, device_id_type=MESH
        )
        return carry

    lax.fori_loop(1, n, greet, 0)
    below = lax.rem(section + sections - 1, sections)
    above = lax.rem(section + 1, sections)
    for neighbour in (below, above):
        for peer in range(parts):
            pl.semaphore_signal(
                barrier,
                inc=1,
                device_id={"pipe": neighbour, "tensor": peer},
                device_id_type=MESH,
            )

    lane = lax.broadcasted_iota(jnp.int32, (1, 128), 1)
    row = jnp.zeros((1, 128), jnp.int32)
    for c in range(2):
        for h in range(heads):
            row = jnp.where(lane == ids[c, h] + c * n, h, row)
    want[...] = row
    table[0] = row

    pl.semaphore_wait(barrier, n - 1 + 2 * parts)

    def tell(step, carry):
        pltpu.make_async_remote_copy(
            src_ref=want,
            dst_ref=table.at[n - step],
            send_sem=want_sem.at[0],
            recv_sem=want_sem.at[1],
            device_id={"dp": ring(me + step)},
            device_id_type=MESH,
        ).start()
        return carry

    lax.fori_loop(1, n, tell, 0)

    def hop(direction, step, c):
        source = own[c] if step == 0 else halo[direction][step - 1][c]
        return pltpu.make_async_remote_copy(
            src_ref=source,
            dst_ref=halo[direction][step][c],
            send_sem=halo_send_sem.at[direction, step, c],
            recv_sem=halo_recv_sem.at[direction, step, c],
            device_id={"dp": ring(me + (1 if direction == 0 else -1))},
            device_id_type=MESH,
        )

    for c in range(2):
        for h in range(heads):
            own_load(c, h).wait()
        for direction in range(2):
            hop(direction, 0, c).start()
    for load in loads:
        load.start()

    rest = table.at[pl.ds(1, n - 1)]
    pltpu.make_async_copy(rest, rest, want_sem.at[1]).wait()
    to_smem = pltpu.make_async_copy(table, table_s, load_sem.at[4])
    to_smem.start()
    to_smem.wait()

    def push(source, destination, direction, distance, c, sem):
        pltpu.make_async_remote_copy(
            src_ref=source,
            dst_ref=destination,
            send_sem=tile_sem.at[sem],
            recv_sem=tile_recv_sem.at[c],
            device_id={"dp": ring(me + (1 - 2 * direction) * distance)},
            device_id_type=MESH,
        ).start()

    def serve(c):
        sources = [ring(me - reach), ring(me + reach)]

        def picked(direction, distance):
            asker = ring((1 - 2 * direction) * distance)
            return table_s[asker, 0, c * n + sources[direction]]

        for direction in range(2):
            head = picked(direction, full + 1)
            send_half[direction, c] = halo[direction][reach - 1][c][head][direction]
            push(
                send_half.at[direction, c],
                recv[c].at[sources[direction], direction],
                direction,
                full + 1,
                c,
                1,
            )

        def one(step, carry):
            distance = full - step
            for direction in range(2):
                head = picked(direction, distance)
                send[direction, c, distance - 1] = halo[direction][reach - 1][c][head]
                push(
                    send.at[direction, c, distance - 1],
                    recv[c].at[sources[direction]],
                    direction,
                    distance,
                    c,
                    0,
                )
            return carry

        lax.fori_loop(0, full, one, 0)

    for step in range(reach):
        for c in range(2):
            for direction in range(2):
                hop(direction, step, c).wait_recv()
                if step < reach - 1:
                    hop(direction, step + 1, c).start()
            if step == reach - 1:
                serve(c)

    for c in range(2):
        for offset in range(-reach, reach + 1):
            block = ring(me + offset)
            head = table_s[0, 0, c * n + block]
            if offset == 0:
                recv[c][block] = own[c][head]
            else:
                recv[c][block] = halo[int(offset > 0)][abs(offset) - 1][c][head]

    for load in loads:
        load.wait()

    def alive(block, live):
        return jnp.clip(live - block, 0, 1).astype(jnp.float32)

    def bias(valid):
        return (valid - 1.0) * HIDDEN

    def score(query, key):
        return (
            lax.dot_general(
                query, key, (((1,), (1,)), ((), ())), preferred_element_type=jnp.float32
            )
            * scale
        )

    def gather(weight, value):
        return jnp.dot(weight.astype(jnp.bfloat16), value, preferred_element_type=jnp.float32)

    for c in range(2):
        live = lens[c]
        bias_before = bias(alive(me - 1, live) * jnp.clip(me, 0, 1).astype(jnp.float32))
        bias_own = bias(alive(me, live))
        bias_after = bias(alive(me + 1, live))

        def near(step, carry):
            for k in range(group):
                h = step * group + k
                cols = pl.ds(pl.multiple_of(h * HD, HD), HD)
                query = q_v[c, :, cols]
                s_before = score(query, halo[0][0][c][h, 0]) + bias_before
                s_own = score(query, own[c][h, 0]) + bias_own
                s_after = score(query, halo[1][0][c][h, 0]) + bias_after
                s_glob = score(query, glob_v[0, c, :, cols])
                largest = jnp.max(jnp.maximum(jnp.maximum(s_before, s_own), s_after), axis=1, keepdims=True)
                largest = jnp.maximum(largest, jnp.max(s_glob, axis=1, keepdims=True))
                w_before = jnp.exp(s_before - largest)
                w_own = jnp.exp(s_own - largest)
                w_after = jnp.exp(s_after - largest)
                w_glob = jnp.exp(s_glob - largest)
                total = jnp.sum(w_before + w_own + w_after, axis=1, keepdims=True)
                total = total + jnp.sum(w_glob, axis=1, keepdims=True)
                context = gather(w_glob, glob_v[1, c, :, cols])
                context = context + gather(w_before, halo[0][0][c][h, 1])
                context = context + gather(w_own, own[c][h, 1])
                context = context + gather(w_after, halo[1][0][c][h, 1])
                acc[c, h] = context
                row_max[c, h] = jnp.broadcast_to(largest, (BLK, HD))
                row_sum[c, h] = jnp.broadcast_to(total, (BLK, HD))
            return carry

        lax.fori_loop(0, heads // group, near, 0)

    def stream_of(c):
        return pltpu.make_async_remote_copy(
            src_ref=upd.at[c],
            dst_ref=arrived.at[c],
            send_sem=out_sem.at[c, parts],
            recv_sem=in_sem.at[c, parts],
            device_id={"pipe": below if c == 0 else above},
            device_id_type=MESH,
        )

    def onward(c):
        target = below if c == 0 else above
        copies = [stream_of(c)]
        for peer in range(parts):
            copies.append(
                pltpu.make_async_remote_copy(
                    src_ref=squares.at[c],
                    dst_ref=squares_in.at[c, part],
                    send_sem=out_sem.at[c, peer],
                    recv_sem=in_sem.at[c, 0],
                    device_id={"pipe": target, "tensor": peer},
                    device_id_type=MESH,
                )
            )
        return copies

    for c in range(2):
        tiles = recv[c].at[pl.ds(0, n - 2 * reach - 1)]
        pltpu.make_async_copy(tiles, tiles, tile_recv_sem.at[c]).wait()
        live = lens[c]
        shown = alive(me, live)

        def far(step, total_squares):
            for k in range(group):
                h = step * group + k
                cols = pl.ds(pl.multiple_of(h * HD, HD), HD)
                block = ids[c, h]
                tile = recv[c][block]
                s_far = score(q_v[c, :, cols], tile[0]) + bias(alive(block, live))
                old = row_max[c, h]
                largest = jnp.maximum(old, jnp.max(s_far, axis=1, keepdims=True))
                shrink = jnp.exp(old - largest)
                w_far = jnp.exp(s_far - largest[:, :BLK])
                total = row_sum[c, h] * shrink + jnp.sum(w_far, axis=1, keepdims=True)
                context = (acc[c, h] * shrink + gather(w_far, tile[1])) / total
                state = res_v[c, :, cols].astype(jnp.float32) + context * shown
                state = state.astype(jnp.bfloat16)
                upd[c, :, cols] = state
                wide = state.astype(jnp.float32)
                total_squares = total_squares + wide * wide
            return total_squares

        squares[c] = lax.fori_loop(
            0, heads // group, far, jnp.zeros((BLK, HD), jnp.float32)
        )
        for copy in onward(c):
            copy.start()

    features = parts * heads * HD
    for c in range(2):
        stream_of(c).wait_recv()
        pltpu.make_async_copy(squares_in.at[c], squares_in.at[c], in_sem.at[c, 0]).wait()
        total = squares_in[c, 0]
        for peer in range(1, parts):
            total = total + squares_in[c, peer]
        inverse = lax.rsqrt(jnp.sum(total, axis=1, keepdims=True) / features + EPSILON)
        edge = section < sections - 1 if c == 0 else section > 0
        kept = jnp.where(edge, 1.0, 0.0).astype(jnp.float32)
        wide = arrived[c].astype(jnp.float32) * kept
        gains = gain_v[pl.ds(c, 1), :].astype(jnp.float32)
        out[c] = (wide * inverse * gains).astype(jnp.bfloat16)

    pltpu.make_async_copy(rest, rest, want_sem.at[0]).wait()
    pltpu.make_async_copy(send, send, tile_sem.at[0]).wait()
    pltpu.make_async_copy(send_half, send_half, tile_sem.at[1]).wait()
    for c in range(2):
        for step in range(reach):
            for direction in range(2):
                hop(direction, step, c).wait_send()
        for copy in onward(c):
            copy.wait_send()


def body(residual, queries, keys_values, global_kv, block_ids, lengths, gain):
    n = lax.axis_size("dp")
    parts = lax.axis_size("tensor")
    width = residual.shape[-1]
    heads = width // HD
    glob = global_kv.shape[3]
    reach = REACH
    full = n // 2 - reach - 1
    stream = (2, BLK, width)
    bf16, f32 = jnp.bfloat16, jnp.float32
    anywhere = pl.BlockSpec(memory_space=pl.ANY)
    scalars = pl.BlockSpec(memory_space=pltpu.SMEM)
    block = pltpu.VMEM((heads, 2, BLK, HD), bf16)
    normed = pl.pallas_call(
        functools.partial(kernel, reach),
        out_shape=jax.ShapeDtypeStruct(stream, bf16),
        in_specs=[scalars, scalars] + [anywhere] * 5,
        out_specs=pl.BlockSpec(memory_space=pltpu.VMEM),
        scratch_shapes=[
            [block] * 2,
            [[[block] * 2 for _ in range(reach)] for _ in range(2)],
            pltpu.VMEM(stream, bf16),
            pltpu.VMEM((2, 2, glob, width), bf16),
            pltpu.VMEM(stream, bf16),
            pltpu.VMEM((2, width), bf16),
            pltpu.VMEM((1, 128), jnp.int32),
            pltpu.VMEM((n, 1, 128), jnp.int32),
            pltpu.SMEM((n, 1, 128), jnp.int32),
            pltpu.VMEM((2, 2, full, 2, BLK, HD), bf16),
            pltpu.VMEM((2, 2, BLK, HD), bf16),
            [pltpu.VMEM((n, 2, BLK, HD), bf16)] * 2,
            pltpu.VMEM((2, heads, BLK, HD), f32),
            pltpu.VMEM((2, heads, BLK, HD), f32),
            pltpu.VMEM((2, heads, BLK, HD), f32),
            pltpu.VMEM(stream, bf16),
            pltpu.VMEM((2, BLK, HD), f32),
            pltpu.VMEM(stream, bf16),
            pltpu.VMEM((2, parts, BLK, HD), f32),
            pltpu.SemaphoreType.DMA((2, heads)),
            pltpu.SemaphoreType.DMA((5,)),
            pltpu.SemaphoreType.DMA((2,)),
            pltpu.SemaphoreType.DMA((2, reach, 2)),
            pltpu.SemaphoreType.DMA((2, reach, 2)),
            pltpu.SemaphoreType.DMA((2,)),
            pltpu.SemaphoreType.DMA((2,)),
            pltpu.SemaphoreType.DMA((2, parts + 1)),
            pltpu.SemaphoreType.DMA((2, parts + 1)),
        ],
        compiler_params=pltpu.CompilerParams(
            collective_id=0, has_side_effects=True, vmem_limit_bytes=48 << 20
        ),
        name="relay_step",
    )(
        block_ids.reshape(2, heads),
        lengths.reshape(2),
        residual,
        queries,
        keys_values,
        global_kv,
        gain,
    )
    return normed[None]


def solution(mesh):
    in_specs = (
        P("pipe", None, "dp", "tensor"),
        P("pipe", None, "dp", "tensor"),
        P("pipe", None, None, "dp", "tensor"),
        P("pipe", None, None, None, "tensor"),
        P("pipe", None, "dp", "tensor"),
        P("pipe", None),
        P("pipe", None, "tensor"),
    )
    out_specs = P("pipe", None, "dp", "tensor")
    return jax.shard_map(body, mesh=mesh, in_specs=in_specs, out_specs=out_specs, check_vma=False)
```

```python
import functools

import jax
import jax.numpy as jnp
from jax import lax
from jax.experimental import pallas as pl
from jax.experimental.pallas import tpu as pltpu
from jax.sharding import PartitionSpec as P

HD = 128
BLK = 64
EPSILON = 1e-05
REACH = 4
HIDDEN = 1e30
GROUP = 4
MESH = pl.DeviceIdType.MESH


def kernel(
    reach,
    ids,
    lens,
    res_hbm,
    q_hbm,
    kv_hbm,
    glob_hbm,
    gain_hbm,
    out,
    own,
    halo,
    q_v,
    glob_v,
    res_v,
    gain_v,
    table,
    table_s,
    send,
    send_half,
    recv,
    acc,
    row_max,
    row_sum,
    upd,
    squares,
    arrived,
    squares_in,
    own_sem,
    load_sem,
    want_send_sem,
    want_recv_sem,
    halo_send_sem,
    halo_recv_sem,
    tile_sem,
    tile_recv_sem,
    out_sem,
    in_sem,
):
    n = lax.axis_size("dp")
    sections = lax.axis_size("pipe")
    parts = lax.axis_size("tensor")
    me = lax.axis_index("dp")
    section = lax.axis_index("pipe")
    part = lax.axis_index("tensor")
    heads = q_v.shape[2] // HD
    group = GROUP if heads % GROUP == 0 else 1
    full = n // 2 - reach - 1
    scale = HD ** (-0.5)

    def ring(index):
        return lax.rem(index + 2 * n, n)

    def own_load(c, h):
        return pltpu.make_async_copy(
            kv_hbm.at[0, :, c, :, pl.ds(h * HD, HD)], own[c].at[h], own_sem.at[c, h]
        )

    loads = [
        pltpu.make_async_copy(q_hbm.at[0], q_v, load_sem.at[0]),
        pltpu.make_async_copy(glob_hbm.at[0], glob_v, load_sem.at[1]),
        pltpu.make_async_copy(res_hbm.at[0], res_v, load_sem.at[2]),
        pltpu.make_async_copy(gain_hbm.at[0], gain_v, load_sem.at[3]),
    ]
    for c in range(2):
        for h in range(heads):
            own_load(c, h).start()

    barrier = pltpu.get_barrier_semaphore()
    below = lax.rem(section + sections - 1, sections)
    above = lax.rem(section + 1, sections)
    for step in (1, n - 1):
        pl.semaphore_signal(
            barrier, inc=1, device_id={"dp": ring(me + step)}, device_id_type=MESH
        )
    for neighbour in (below, above):
        for peer in range(parts):
            pl.semaphore_signal(
                barrier,
                inc=1,
                device_id={"pipe": neighbour, "tensor": peer},
                device_id_type=MESH,
            )

    lane = lax.broadcasted_iota(jnp.int32, (1, 128), 1)
    row = jnp.zeros((1, 128), jnp.int32)
    for c in range(2):
        for h in range(heads):
            row = jnp.where(lane == ids[c, h] + c * n, h, row)
    half = n // 2
    table[half] = row

    pl.semaphore_wait(barrier, 2 + 2 * parts)

    rounds = half.bit_length() - 1

    def spread(index, direction):
        count = 1 << index
        if direction == 0:
            source, destination = half - count + 1, half - 2 * count + 1
        else:
            source, destination = half, half + count
        return pltpu.make_async_remote_copy(
            src_ref=table.at[pl.ds(source, count)],
            dst_ref=table.at[pl.ds(destination, count)],
            send_sem=want_send_sem.at[index, direction],
            recv_sem=want_recv_sem.at[index, direction],
            device_id={"dp": ring(me + (1 - 2 * direction) * count)},
            device_id_type=MESH,
        )

    for direction in range(2):
        spread(0, direction).start()

    def hop(direction, step, c):
        source = own[c] if step == 0 else halo[direction][step - 1][c]
        return pltpu.make_async_remote_copy(
            src_ref=source,
            dst_ref=halo[direction][step][c],
            send_sem=halo_send_sem.at[direction, step, c],
            recv_sem=halo_recv_sem.at[direction, step, c],
            device_id={"dp": ring(me + (1 if direction == 0 else -1))},
            device_id_type=MESH,
        )

    for c in range(2):
        for h in range(heads):
            own_load(c, h).wait()
        for direction in range(2):
            hop(direction, 0, c).start()
    for load in loads:
        load.start()

    def push(source, destination, direction, distance, c, sem):
        pltpu.make_async_remote_copy(
            src_ref=source,
            dst_ref=destination,
            send_sem=tile_sem.at[sem],
            recv_sem=tile_recv_sem.at[c],
            device_id={"dp": ring(me + (1 - 2 * direction) * distance)},
            device_id_type=MESH,
        ).start()

    def serve(c):
        sources = [ring(me - reach), ring(me + reach)]

        def picked(direction, distance):
            asker = half + (1 - 2 * direction) * distance
            return table_s[asker, 0, c * n + sources[direction]]

        for direction in range(2):
            head = picked(direction, full + 1)
            send_half[direction, c] = halo[direction][reach - 1][c][head][direction]
            push(
                send_half.at[direction, c],
                recv[c].at[sources[direction], direction],
                direction,
                full + 1,
                c,
                1,
            )

        def one(step, carry):
            distance = full - step
            for direction in range(2):
                head = picked(direction, distance)
                send[direction, c, distance - 1] = halo[direction][reach - 1][c][head]
                push(
                    send.at[direction, c, distance - 1],
                    recv[c].at[sources[direction]],
                    direction,
                    distance,
                    c,
                    0,
                )
            return carry

        lax.fori_loop(0, full, one, 0)

    def advance(index):
        for direction in range(2):
            spread(index, direction).wait_recv()
        if index < rounds - 1:
            for direction in range(2):
                spread(index + 1, direction).start()

    to_come = list(range(rounds))
    advance(to_come.pop(0))
    for step in range(reach):
        for c in range(2):
            for direction in range(2):
                hop(direction, step, c).wait_recv()
                if step < reach - 1:
                    hop(direction, step + 1, c).start()
            if step < reach - 1:
                if to_come:
                    advance(to_come.pop(0))
                continue
            if c == 0:
                while to_come:
                    advance(to_come.pop(0))
                rows = pl.ds(1, n - 1)
                to_smem = pltpu.make_async_copy(
                    table.at[rows], table_s.at[rows], load_sem.at[4]
                )
                to_smem.start()
                to_smem.wait()
            serve(c)

    for c in range(2):
        for offset in range(-reach, reach + 1):
            block = ring(me + offset)
            head = table_s[half, 0, c * n + block]
            if offset == 0:
                recv[c][block] = own[c][head]
            else:
                recv[c][block] = halo[int(offset > 0)][abs(offset) - 1][c][head]

    for load in loads:
        load.wait()

    def alive(block, live):
        return jnp.clip(live - block, 0, 1).astype(jnp.float32)

    def bias(valid):
        return (valid - 1.0) * HIDDEN

    def score(query, key):
        return (
            lax.dot_general(
                query, key, (((1,), (1,)), ((), ())), preferred_element_type=jnp.float32
            )
            * scale
        )

    def gather(weight, value):
        return jnp.dot(weight.astype(jnp.bfloat16), value, preferred_element_type=jnp.float32)

    for c in range(2):
        live = lens[c]
        bias_before = bias(alive(me - 1, live) * jnp.clip(me, 0, 1).astype(jnp.float32))
        bias_own = bias(alive(me, live))
        bias_after = bias(alive(me + 1, live))

        def near(step, carry):
            for k in range(group):
                h = step * group + k
                cols = pl.ds(pl.multiple_of(h * HD, HD), HD)
                query = q_v[c, :, cols]
                s_before = score(query, halo[0][0][c][h, 0]) + bias_before
                s_own = score(query, own[c][h, 0]) + bias_own
                s_after = score(query, halo[1][0][c][h, 0]) + bias_after
                s_glob = score(query, glob_v[0, c, :, cols])
                largest = jnp.max(jnp.maximum(jnp.maximum(s_before, s_own), s_after), axis=1, keepdims=True)
                largest = jnp.maximum(largest, jnp.max(s_glob, axis=1, keepdims=True))
                w_before = jnp.exp(s_before - largest)
                w_own = jnp.exp(s_own - largest)
                w_after = jnp.exp(s_after - largest)
                w_glob = jnp.exp(s_glob - largest)
                total = jnp.sum(w_before + w_own + w_after, axis=1, keepdims=True)
                total = total + jnp.sum(w_glob, axis=1, keepdims=True)
                context = gather(w_glob, glob_v[1, c, :, cols])
                context = context + gather(w_before, halo[0][0][c][h, 1])
                context = context + gather(w_own, own[c][h, 1])
                context = context + gather(w_after, halo[1][0][c][h, 1])
                acc[c, h] = context
                row_max[c, h] = jnp.broadcast_to(largest, (BLK, HD))
                row_sum[c, h] = jnp.broadcast_to(total, (BLK, HD))
            return carry

        lax.fori_loop(0, heads // group, near, 0)

    def stream_of(c):
        return pltpu.make_async_remote_copy(
            src_ref=upd.at[c],
            dst_ref=arrived.at[c],
            send_sem=out_sem.at[c, parts],
            recv_sem=in_sem.at[c, parts],
            device_id={"pipe": below if c == 0 else above},
            device_id_type=MESH,
        )

    def onward(c):
        target = below if c == 0 else above
        copies = [stream_of(c)]
        for peer in range(parts):
            copies.append(
                pltpu.make_async_remote_copy(
                    src_ref=squares.at[c],
                    dst_ref=squares_in.at[c, part],
                    send_sem=out_sem.at[c, peer],
                    recv_sem=in_sem.at[c, 0],
                    device_id={"pipe": target, "tensor": peer},
                    device_id_type=MESH,
                )
            )
        return copies

    for c in range(2):
        tiles = recv[c].at[pl.ds(0, n - 2 * reach - 1)]
        pltpu.make_async_copy(tiles, tiles, tile_recv_sem.at[c]).wait()
        live = lens[c]
        shown = alive(me, live)

        def far(step, total_squares):
            for k in range(group):
                h = step * group + k
                cols = pl.ds(pl.multiple_of(h * HD, HD), HD)
                block = ids[c, h]
                tile = recv[c][block]
                s_far = score(q_v[c, :, cols], tile[0]) + bias(alive(block, live))
                old = row_max[c, h]
                largest = jnp.maximum(old, jnp.max(s_far, axis=1, keepdims=True))
                shrink = jnp.exp(old - largest)
                w_far = jnp.exp(s_far - largest[:, :BLK])
                total = row_sum[c, h] * shrink + jnp.sum(w_far, axis=1, keepdims=True)
                context = (acc[c, h] * shrink + gather(w_far, tile[1])) / total
                state = res_v[c, :, cols].astype(jnp.float32) + context * shown
                state = state.astype(jnp.bfloat16)
                upd[c, :, cols] = state
                wide = state.astype(jnp.float32)
                total_squares = total_squares + wide * wide
            return total_squares

        total_squares = lax.fori_loop(
            0, heads // group, far, jnp.zeros((BLK, HD), jnp.float32)
        )
        squares[c] = lax.dot_general(
            jnp.ones((8, HD), jnp.float32),
            jnp.concatenate([total_squares, total_squares], axis=0),
            (((1,), (1,)), ((), ())),
            precision=lax.Precision.HIGHEST,
            preferred_element_type=jnp.float32,
        )
        for copy in onward(c):
            copy.start()

    features = parts * heads * HD
    for c in range(2):
        stream_of(c).wait_recv()
        pltpu.make_async_copy(squares_in.at[c], squares_in.at[c], in_sem.at[c, 0]).wait()
        total = squares_in[c, 0]
        for peer in range(1, parts):
            total = total + squares_in[c, peer]
        mean = lax.dot_general(
            total[:, :BLK],
            jnp.full((8, HD), 1.0 / 8, jnp.float32),
            (((0,), (0,)), ((), ())),
            precision=lax.Precision.HIGHEST,
            preferred_element_type=jnp.float32,
        )
        inverse = lax.rsqrt(mean[:, :1] / features + EPSILON)
        edge = section < sections - 1 if c == 0 else section > 0
        kept = jnp.where(edge, 1.0, 0.0).astype(jnp.float32)
        wide = arrived[c].astype(jnp.float32) * kept
        gains = gain_v[pl.ds(c, 1), :].astype(jnp.float32)
        out[c] = (wide * inverse * gains).astype(jnp.bfloat16)

    for index in range(rounds):
        for direction in range(2):
            spread(index, direction).wait_send()
    pltpu.make_async_copy(send, send, tile_sem.at[0]).wait()
    pltpu.make_async_copy(send_half, send_half, tile_sem.at[1]).wait()
    for c in range(2):
        for step in range(reach):
            for direction in range(2):
                hop(direction, step, c).wait_send()
        for copy in onward(c):
            copy.wait_send()


def body(residual, queries, keys_values, global_kv, block_ids, lengths, gain):
    n = lax.axis_size("dp")
    parts = lax.axis_size("tensor")
    width = residual.shape[-1]
    heads = width // HD
    glob = global_kv.shape[3]
    reach = REACH
    full = n // 2 - reach - 1
    rounds = (n // 2).bit_length() - 1
    stream = (2, BLK, width)
    bf16, f32 = jnp.bfloat16, jnp.float32
    in_hbm = pl.BlockSpec(memory_space=pltpu.HBM)
    scalars = pl.BlockSpec(memory_space=pltpu.SMEM)
    block = pltpu.VMEM((heads, 2, BLK, HD), bf16)
    normed = pl.pallas_call(
        functools.partial(kernel, reach),
        out_shape=jax.ShapeDtypeStruct(stream, bf16),
        in_specs=[scalars, scalars] + [in_hbm] * 5,
        out_specs=pl.BlockSpec(memory_space=pltpu.VMEM),
        scratch_shapes=[
            [block] * 2,
            [[[block] * 2 for _ in range(reach)] for _ in range(2)],
            pltpu.VMEM(stream, bf16),
            pltpu.VMEM((2, 2, glob, width), bf16),
            pltpu.VMEM(stream, bf16),
            pltpu.VMEM((2, width), bf16),
            pltpu.VMEM((n, 1, 128), jnp.int32),
            pltpu.SMEM((n, 1, 128), jnp.int32),
            pltpu.VMEM((2, 2, full, 2, BLK, HD), bf16),
            pltpu.VMEM((2, 2, BLK, HD), bf16),
            [pltpu.VMEM((n, 2, BLK, HD), bf16)] * 2,
            pltpu.VMEM((2, heads, BLK, HD), f32),
            pltpu.VMEM((2, heads, BLK, HD), f32),
            pltpu.VMEM((2, heads, BLK, HD), f32),
            pltpu.VMEM(stream, bf16),
            pltpu.VMEM((2, 8, HD), f32),
            pltpu.VMEM(stream, bf16),
            pltpu.VMEM((2, parts, 8, HD), f32),
            pltpu.SemaphoreType.DMA((2, heads)),
            pltpu.SemaphoreType.DMA((5,)),
            pltpu.SemaphoreType.DMA((rounds, 2)),
            pltpu.SemaphoreType.DMA((rounds, 2)),
            pltpu.SemaphoreType.DMA((2, reach, 2)),
            pltpu.SemaphoreType.DMA((2, reach, 2)),
            pltpu.SemaphoreType.DMA((2,)),
            pltpu.SemaphoreType.DMA((2,)),
            pltpu.SemaphoreType.DMA((2, parts + 1)),
            pltpu.SemaphoreType.DMA((2, parts + 1)),
        ],
        compiler_params=pltpu.CompilerParams(
            collective_id=0, has_side_effects=True, vmem_limit_bytes=63 << 20
        ),
        name="relay_step",
    )(
        block_ids.reshape(2, heads),
        lengths.reshape(2),
        residual,
        queries,
        keys_values,
        global_kv,
        gain,
    )
    return normed[None]


def solution(mesh):
    in_specs = (
        P("pipe", None, "dp", "tensor"),
        P("pipe", None, "dp", "tensor"),
        P("pipe", None, None, "dp", "tensor"),
        P("pipe", None, None, None, "tensor"),
        P("pipe", None, "dp", "tensor"),
        P("pipe", None),
        P("pipe", None, "tensor"),
    )
    out_specs = P("pipe", None, "dp", "tensor")
    return jax.shard_map(body, mesh=mesh, in_specs=in_specs, out_specs=out_specs, check_vma=False)
```

```python
import functools

import jax
import jax.numpy as jnp
from jax import lax
from jax.experimental import pallas as pl
from jax.experimental.pallas import tpu as pltpu
from jax.sharding import PartitionSpec as P

HD = 128
BLK = 64
EPSILON = 1e-05
REACH = 4
HIDDEN = 1e30
GROUP = 4
MESH = pl.DeviceIdType.MESH


def kernel(
    reach,
    ids,
    lens,
    res_hbm,
    q_hbm,
    kv_hbm,
    glob_hbm,
    gain_hbm,
    out,
    own,
    halo,
    q_v,
    glob_v,
    res_v,
    gain_v,
    table,
    table_s,
    send,
    send_half,
    recv,
    acc,
    row_max,
    row_sum,
    upd,
    squares,
    arrived,
    squares_in,
    own_sem,
    load_sem,
    want_send_sem,
    want_recv_sem,
    halo_send_sem,
    halo_recv_sem,
    tile_sem,
    tile_recv_sem,
    stream_send_sem,
    stream_recv_sem,
    squares_send_sem,
    squares_recv_sem,
):
    n = lax.axis_size("dp")
    sections = lax.axis_size("pipe")
    parts = lax.axis_size("tensor")
    me = lax.axis_index("dp")
    section = lax.axis_index("pipe")
    part = lax.axis_index("tensor")
    heads = q_v.shape[2] // HD
    group = GROUP if heads % GROUP == 0 else 1
    full = n // 2 - reach - 1
    scale = HD ** (-0.5)

    def ring(index):
        return lax.rem(index + 2 * n, n)

    def own_load(c, h):
        return pltpu.make_async_copy(
            kv_hbm.at[0, :, c, :, pl.ds(h * HD, HD)], own[c].at[h], own_sem.at[c, h]
        )

    loads = [
        pltpu.make_async_copy(q_hbm.at[0], q_v, load_sem.at[0]),
        pltpu.make_async_copy(glob_hbm.at[0], glob_v, load_sem.at[1]),
        pltpu.make_async_copy(res_hbm.at[0], res_v, load_sem.at[2]),
        pltpu.make_async_copy(gain_hbm.at[0], gain_v, load_sem.at[3]),
    ]
    for c in range(2):
        for h in range(heads):
            own_load(c, h).start()

    barrier = pltpu.get_barrier_semaphore()
    below = lax.rem(section + sections - 1, sections)
    above = lax.rem(section + 1, sections)
    for step in (1, n - 1):
        pl.semaphore_signal(
            barrier, inc=1, device_id={"dp": ring(me + step)}, device_id_type=MESH
        )
    for neighbour in (below, above):
        for peer in range(parts):
            pl.semaphore_signal(
                barrier,
                inc=1,
                device_id={"pipe": neighbour, "tensor": peer},
                device_id_type=MESH,
            )

    lane = lax.broadcasted_iota(jnp.int32, (1, 128), 1)
    row = jnp.zeros((1, 128), jnp.int32)
    for c in range(2):
        for h in range(heads):
            row = jnp.where(lane == ids[c, h] + c * n, h, row)
    half = n // 2
    table[half] = row

    pl.semaphore_wait(barrier, 2 + 2 * parts)

    rounds = half.bit_length() - 1

    def spread(index, direction):
        count = 1 << index
        if direction == 0:
            source, destination = half - count + 1, half - 2 * count + 1
        else:
            source, destination = half, half + count
        return pltpu.make_async_remote_copy(
            src_ref=table.at[pl.ds(source, count)],
            dst_ref=table.at[pl.ds(destination, count)],
            send_sem=want_send_sem.at[index, direction],
            recv_sem=want_recv_sem.at[index, direction],
            device_id={"dp": ring(me + (1 - 2 * direction) * count)},
            device_id_type=MESH,
        )

    for direction in range(2):
        spread(0, direction).start()

    def hop(direction, step, c):
        source = own[c] if step == 0 else halo[direction][step - 1][c]
        return pltpu.make_async_remote_copy(
            src_ref=source,
            dst_ref=halo[direction][step][c],
            send_sem=halo_send_sem.at[direction, step, c],
            recv_sem=halo_recv_sem.at[direction, step, c],
            device_id={"dp": ring(me + (1 if direction == 0 else -1))},
            device_id_type=MESH,
        )

    for c in range(2):
        for h in range(heads):
            own_load(c, h).wait()
        for direction in range(2):
            hop(direction, 0, c).start()
    for load in loads:
        load.start()

    def push(source, destination, direction, distance, c, sem):
        pltpu.make_async_remote_copy(
            src_ref=source,
            dst_ref=destination,
            send_sem=tile_sem.at[sem],
            recv_sem=tile_recv_sem.at[c],
            device_id={"dp": ring(me + (1 - 2 * direction) * distance)},
            device_id_type=MESH,
        ).start()

    def serve(c):
        sources = [ring(me - reach), ring(me + reach)]

        def picked(direction, distance):
            asker = half + (1 - 2 * direction) * distance
            return table_s[asker, 0, c * n + sources[direction]]

        for direction in range(2):
            head = picked(direction, full + 1)
            send_half[direction, c] = halo[direction][reach - 1][c][head][direction]
            push(
                send_half.at[direction, c],
                recv[c].at[sources[direction], direction],
                direction,
                full + 1,
                c,
                1,
            )

        def one(step, carry):
            distance = full - step
            for direction in range(2):
                head = picked(direction, distance)
                send[direction, c, distance - 1] = halo[direction][reach - 1][c][head]
                push(
                    send.at[direction, c, distance - 1],
                    recv[c].at[sources[direction]],
                    direction,
                    distance,
                    c,
                    0,
                )
            return carry

        lax.fori_loop(0, full, one, 0)

    def advance(index):
        for direction in range(2):
            spread(index, direction).wait_recv()
        if index < rounds - 1:
            for direction in range(2):
                spread(index + 1, direction).start()

    to_come = list(range(rounds))
    for step in range(reach):
        for c in range(2):
            hop(0, step, c).wait_recv()
            if c == 0 and to_come:
                advance(to_come.pop(0))
            if step < reach - 1:
                hop(0, step + 1, c).start()
            hop(1, step, c).wait_recv()
            if step < reach - 1:
                hop(1, step + 1, c).start()
                continue
            if c == 0:
                while to_come:
                    advance(to_come.pop(0))
                rows = pl.ds(1, n - 1)
                to_smem = pltpu.make_async_copy(
                    table.at[rows], table_s.at[rows], load_sem.at[4]
                )
                to_smem.start()
                to_smem.wait()
            serve(c)

    for c in range(2):
        for offset in range(-reach, reach + 1):
            block = ring(me + offset)
            head = table_s[half, 0, c * n + block]
            if offset == 0:
                recv[c][block] = own[c][head]
            else:
                recv[c][block] = halo[int(offset > 0)][abs(offset) - 1][c][head]

    for load in loads:
        load.wait()

    def alive(block, live):
        return jnp.clip(live - block, 0, 1).astype(jnp.float32)

    def bias(valid):
        return (valid - 1.0) * HIDDEN

    def score(query, key):
        return (
            lax.dot_general(
                query, key, (((1,), (1,)), ((), ())), preferred_element_type=jnp.float32
            )
            * scale
        )

    def gather(weight, value):
        return jnp.dot(weight.astype(jnp.bfloat16), value, preferred_element_type=jnp.float32)

    for c in range(2):
        live = lens[c]
        bias_before = bias(alive(me - 1, live) * jnp.clip(me, 0, 1).astype(jnp.float32))
        bias_own = bias(alive(me, live))
        bias_after = bias(alive(me + 1, live))

        def near(step, carry):
            for k in range(group):
                h = step * group + k
                cols = pl.ds(pl.multiple_of(h * HD, HD), HD)
                query = q_v[c, :, cols]
                s_before = score(query, halo[0][0][c][h, 0]) + bias_before
                s_own = score(query, own[c][h, 0]) + bias_own
                s_after = score(query, halo[1][0][c][h, 0]) + bias_after
                s_glob = score(query, glob_v[0, c, :, cols])
                largest = jnp.max(jnp.maximum(jnp.maximum(s_before, s_own), s_after), axis=1, keepdims=True)
                largest = jnp.maximum(largest, jnp.max(s_glob, axis=1, keepdims=True))
                w_before = jnp.exp(s_before - largest)
                w_own = jnp.exp(s_own - largest)
                w_after = jnp.exp(s_after - largest)
                w_glob = jnp.exp(s_glob - largest)
                total = jnp.sum(w_before + w_own + w_after, axis=1, keepdims=True)
                total = total + jnp.sum(w_glob, axis=1, keepdims=True)
                context = gather(w_glob, glob_v[1, c, :, cols])
                context = context + gather(w_before, halo[0][0][c][h, 1])
                context = context + gather(w_own, own[c][h, 1])
                context = context + gather(w_after, halo[1][0][c][h, 1])
                acc[c, h] = context
                row_max[c, h] = jnp.broadcast_to(largest, (BLK, HD))
                row_sum[c, h] = jnp.broadcast_to(total, (BLK, HD))
            return carry

        lax.fori_loop(0, heads // group, near, 0)

    def stream_of(c, step):
        cols = pl.ds(pl.multiple_of(step * group * HD, HD), group * HD)
        return pltpu.make_async_remote_copy(
            src_ref=upd.at[c, :, cols],
            dst_ref=arrived.at[c, :, cols],
            send_sem=stream_send_sem.at[c, step],
            recv_sem=stream_recv_sem.at[c, step],
            device_id={"pipe": below if c == 0 else above},
            device_id_type=MESH,
        )

    def squares_of(c, peer):
        return pltpu.make_async_remote_copy(
            src_ref=squares.at[c],
            dst_ref=squares_in.at[c, part],
            send_sem=squares_send_sem.at[c, peer],
            recv_sem=squares_recv_sem.at[c],
            device_id={"pipe": below if c == 0 else above, "tensor": peer},
            device_id_type=MESH,
        )

    for c in range(2):
        tiles = recv[c].at[pl.ds(0, n - 2 * reach - 1)]
        pltpu.make_async_copy(tiles, tiles, tile_recv_sem.at[c]).wait()
        live = lens[c]
        shown = alive(me, live)

        def far(step, total_squares):
            for k in range(group):
                h = step * group + k
                cols = pl.ds(pl.multiple_of(h * HD, HD), HD)
                block = ids[c, h]
                tile = recv[c][block]
                s_far = score(q_v[c, :, cols], tile[0]) + bias(alive(block, live))
                old = row_max[c, h]
                largest = jnp.maximum(old, jnp.max(s_far, axis=1, keepdims=True))
                shrink = jnp.exp(old - largest)
                w_far = jnp.exp(s_far - largest[:, :BLK])
                total = row_sum[c, h] * shrink + jnp.sum(w_far, axis=1, keepdims=True)
                context = (acc[c, h] * shrink + gather(w_far, tile[1])) / total
                state = res_v[c, :, cols].astype(jnp.float32) + context * shown
                state = state.astype(jnp.bfloat16)
                upd[c, :, cols] = state
                wide = state.astype(jnp.float32)
                total_squares = total_squares + wide * wide
            stream_of(c, step).start()
            return total_squares

        total_squares = lax.fori_loop(
            0, heads // group, far, jnp.zeros((BLK, HD), jnp.float32)
        )
        squares[c] = lax.dot_general(
            jnp.ones((8, HD), jnp.float32),
            jnp.concatenate([total_squares, total_squares], axis=0),
            (((1,), (1,)), ((), ())),
            precision=lax.Precision.HIGHEST,
            preferred_element_type=jnp.float32,
        )
        for peer in range(parts):
            squares_of(c, peer).start()

    features = parts * heads * HD
    for c in range(2):
        for step in range(heads // group):
            stream_of(c, step).wait_recv()
        pltpu.make_async_copy(squares_in.at[c], squares_in.at[c], squares_recv_sem.at[c]).wait()
        total = squares_in[c, 0]
        for peer in range(1, parts):
            total = total + squares_in[c, peer]
        mean = lax.dot_general(
            total[:, :BLK],
            jnp.full((8, HD), 1.0 / 8, jnp.float32),
            (((0,), (0,)), ((), ())),
            precision=lax.Precision.HIGHEST,
            preferred_element_type=jnp.float32,
        )
        inverse = lax.rsqrt(mean[:, :1] / features + EPSILON)
        edge = section < sections - 1 if c == 0 else section > 0
        kept = jnp.where(edge, 1.0, 0.0).astype(jnp.float32)
        wide = arrived[c].astype(jnp.float32) * kept
        gains = gain_v[pl.ds(c, 1), :].astype(jnp.float32)
        out[c] = (wide * inverse * gains).astype(jnp.bfloat16)

    for index in range(rounds):
        for direction in range(2):
            spread(index, direction).wait_send()
    pltpu.make_async_copy(send, send, tile_sem.at[0]).wait()
    pltpu.make_async_copy(send_half, send_half, tile_sem.at[1]).wait()
    for c in range(2):
        for step in range(reach):
            for direction in range(2):
                hop(direction, step, c).wait_send()
        for step in range(heads // group):
            stream_of(c, step).wait_send()
        for peer in range(parts):
            squares_of(c, peer).wait_send()


def body(residual, queries, keys_values, global_kv, block_ids, lengths, gain):
    n = lax.axis_size("dp")
    parts = lax.axis_size("tensor")
    width = residual.shape[-1]
    heads = width // HD
    glob = global_kv.shape[3]
    reach = REACH
    full = n // 2 - reach - 1
    rounds = (n // 2).bit_length() - 1
    stream = (2, BLK, width)
    bf16, f32 = jnp.bfloat16, jnp.float32
    in_hbm = pl.BlockSpec(memory_space=pltpu.HBM)
    scalars = pl.BlockSpec(memory_space=pltpu.SMEM)
    block = pltpu.VMEM((heads, 2, BLK, HD), bf16)
    normed = pl.pallas_call(
        functools.partial(kernel, reach),
        out_shape=jax.ShapeDtypeStruct(stream, bf16),
        in_specs=[scalars, scalars] + [in_hbm] * 5,
        out_specs=pl.BlockSpec(memory_space=pltpu.VMEM),
        scratch_shapes=[
            [block] * 2,
            [[[block] * 2 for _ in range(reach)] for _ in range(2)],
            pltpu.VMEM(stream, bf16),
            pltpu.VMEM((2, 2, glob, width), bf16),
            pltpu.VMEM(stream, bf16),
            pltpu.VMEM((2, width), bf16),
            pltpu.VMEM((n, 1, 128), jnp.int32),
            pltpu.SMEM((n, 1, 128), jnp.int32),
            pltpu.VMEM((2, 2, full, 2, BLK, HD), bf16),
            pltpu.VMEM((2, 2, BLK, HD), bf16),
            [pltpu.VMEM((n, 2, BLK, HD), bf16)] * 2,
            pltpu.VMEM((2, heads, BLK, HD), f32),
            pltpu.VMEM((2, heads, BLK, HD), f32),
            pltpu.VMEM((2, heads, BLK, HD), f32),
            pltpu.VMEM(stream, bf16),
            pltpu.VMEM((2, 8, HD), f32),
            pltpu.VMEM(stream, bf16),
            pltpu.VMEM((2, parts, 8, HD), f32),
            pltpu.SemaphoreType.DMA((2, heads)),
            pltpu.SemaphoreType.DMA((5,)),
            pltpu.SemaphoreType.DMA((rounds, 2)),
            pltpu.SemaphoreType.DMA((rounds, 2)),
            pltpu.SemaphoreType.DMA((2, reach, 2)),
            pltpu.SemaphoreType.DMA((2, reach, 2)),
            pltpu.SemaphoreType.DMA((2,)),
            pltpu.SemaphoreType.DMA((2,)),
            pltpu.SemaphoreType.DMA((2, heads)),
            pltpu.SemaphoreType.DMA((2, heads)),
            pltpu.SemaphoreType.DMA((2, parts)),
            pltpu.SemaphoreType.DMA((2,)),
        ],
        compiler_params=pltpu.CompilerParams(
            collective_id=0, has_side_effects=True, vmem_limit_bytes=63 << 20
        ),
        name="relay_step",
    )(
        block_ids.reshape(2, heads),
        lengths.reshape(2),
        residual,
        queries,
        keys_values,
        global_kv,
        gain,
    )
    return normed[None]


def solution(mesh):
    in_specs = (
        P("pipe", None, "dp", "tensor"),
        P("pipe", None, "dp", "tensor"),
        P("pipe", None, None, "dp", "tensor"),
        P("pipe", None, None, None, "tensor"),
        P("pipe", None, "dp", "tensor"),
        P("pipe", None),
        P("pipe", None, "tensor"),
    )
    out_specs = P("pipe", None, "dp", "tensor")
    return jax.shard_map(body, mesh=mesh, in_specs=in_specs, out_specs=out_specs, check_vma=False)
```
